32 devices in a mesh: rep: 16 (over z, x, core), grp: 2 (over y).
Axes of the slice: x: 2, y: 2, z: 4, core: 2. Of those that a mesh axis runs over, the one named last changes fastest.
Arguments:
- stream_in: float32 [16, 256, 1024], P('rep', 'grp'), may hold values from -6 to 6
- first_norm_gain: bfloat16 [1024], P('grp'), may hold values from 0.099609375 to 1.8984375
- first_norm_bias: bfloat16 [1024], P('grp'), may hold values from -3 to 3
- w_qkv: bfloat16 [1024, 3072], P('grp'), may hold values from -6 to 6, as said below
- bias_q: bfloat16 [1024], P('grp'), may hold values from -3 to 3
- bias_v: bfloat16 [1024], P('grp'), may hold values from -3 to 3
- w_out: bfloat16 [1024, 1024], P('grp'), may hold values from -0.75 to 0.75
- bias_out: bfloat16 [1024], P('grp'), may hold values from -3 to 3
- second_norm_gain: bfloat16 [1024], P('grp'), may hold values from 0.099609375 to 1.8984375
- second_norm_bias: bfloat16 [1024], P('grp'), may hold values from -3 to 3
- w_up: bfloat16 [1024, 4096], P('grp'), may hold values from -0.1875 to 0.1875
- bias_up: bfloat16 [4096], P('grp'), may hold values from -3 to 3
- w_down: bfloat16 [4096, 1024], P('grp'), may hold values from -0.09375 to 0.09375
- bias_down: bfloat16 [1024], P('grp'), may hold values from -3 to 3
- cotangent: float32 [16, 256, 1024], P('rep', 'grp'), may hold values from -6 to 6
Outputs:
- stream_out: float32 [16, 256, 1024], P('rep', 'grp')
- stream_grad: float32 [16, 256, 1024], P('rep', 'grp')
- ln1_gain_grad: float32 [1024], P('grp')
- ln1_bias_grad: float32 [1024], P('grp')
- w_qkv_grad: float32 [1024, 3072], P('grp')
- bias_q_grad: float32 [1024], P('grp')
- bias_v_grad: float32 [1024], P('grp')
- w_out_grad: float32 [1024, 1024], P('grp')
- bias_out_grad: float32 [1024], P('grp')
- ln2_gain_grad: float32 [1024], P('grp')
- ln2_bias_grad: float32 [1024], P('grp')
- w_up_grad: float32 [1024, 4096], P('grp')
- bias_up_grad: float32 [4096], P('grp')
- w_down_grad: float32 [4096, 1024], P('grp')
- bias_down_grad: float32 [1024], P('grp')
The draws below stay inside these ranges and needn't reach their ends.
Inputs may be any that keep to these rules, and one draw needn't show every extreme that they name: `w_qkv`: the columns hold the query, key and value projections in that order.
All inputs are finite; a program needn't handle non-finite values.
Results may differ from the reference program's by a relative error of at most 0.018.
Values may be sent and summed in bfloat16 or wider, within the bound.
A program may use at most 192 MiB of HBM per device.

```python
import math
import jax
import jax.numpy as jnp
from jax import lax

D = 1024
HEADS = 16
HEAD_DIM = 64
FF = 4096
SEQ_LEN = 256
SEQS = 16


def draw_w_qkv(key, part):
    drawn_all = jnp.clip(jax.random.normal(key, (D, 3 * D), jnp.float32), -5.0, 5.0) * D ** (-0.5)
    return drawn_all.astype(jnp.bfloat16)


def block_scale(own_key, shape, pieces, low, largest):
    loudness, own = 1.0, jax.random.fold_in(own_key, 6)
    for axis_at, blocks in pieces:
        heights = jnp.exp(jax.random.uniform(jax.random.fold_in(own, axis_at), (blocks,), jnp.float32, low / len(pieces), largest / len(pieces)))
        loudness = loudness * jnp.repeat(heights, shape[axis_at] // blocks).reshape([-1 if axis == axis_at else 1 for axis in range(len(shape))])
    return loudness


def gaussian(key, shape, scale, reach, pieces=(), kind=jnp.bfloat16):
    array = jax.random.normal(key, shape, jnp.float32) * scale
    if len(pieces) > 0:
        array = block_scale(key, shape, pieces, -0.22, 0.18) * array
    return jnp.clip(array, min=-reach, max=reach).astype(kind)


def setup_inputs(seed: int = 0) -> dict:
    key_list = jax.random.split(jax.random.key(seed), 16)
    stream_in = gaussian(key_list[0], (SEQS, SEQ_LEN, D), 1.0, 6.0, ((0, 16), (1, 2)), jnp.float32)
    first_norm_gain = jnp.clip(1.0 + 0.18 * jax.random.normal(key_list[1], (D,), jnp.float32), 0.099609375, 1.8984375).astype(jnp.bfloat16)
    first_norm_bias = gaussian(key_list[2], (D,), 0.5, 3.0, ((0, 2),))
    w_qkv = draw_w_qkv(jax.random.fold_in(key_list[15], 71), 0)
    bias_q = gaussian(key_list[4], (D,), 0.5, 3.0, ((0, 2),))
    bias_v = gaussian(key_list[5], (D,), 0.5, 3.0, ((0, 2),))
    w_out = gaussian(key_list[6], (D, D), (D // 16) ** -0.5, 0.75, ((0, 2),))
    bias_out = gaussian(key_list[7], (D,), 0.5, 3.0, ((0, 2),))
    second_norm_gain = jnp.clip(1.0 + 0.18 * jax.random.normal(key_list[8], (D,), jnp.float32), 0.099609375, 1.8984375).astype(jnp.bfloat16)
    second_norm_bias = gaussian(key_list[9], (D,), 0.5, 3.0, ((0, 2),))
    w_up = gaussian(key_list[10], (D, FF), D ** -0.5, 0.1875, ((0, 2),))
    bias_up = gaussian(key_list[11], (FF,), 0.5, 3.0, ((0, 2),))
    w_down = gaussian(key_list[12], (FF, D), FF ** -0.5, 0.09375, ((0, 2),))
    bias_down = gaussian(key_list[13], (D,), 0.5, 3.0, ((0, 2),))
    cotangent = gaussian(key_list[14], (SEQS, SEQ_LEN, D), 1.0, 6.0, ((0, 16), (1, 2)), jnp.float32)
    return dict(stream_in=stream_in, first_norm_gain=first_norm_gain, first_norm_bias=first_norm_bias, w_qkv=w_qkv, bias_q=bias_q, bias_v=bias_v, w_out=w_out, bias_out=bias_out, second_norm_gain=second_norm_gain, second_norm_bias=second_norm_bias, w_up=w_up, bias_up=bias_up, w_down=w_down, bias_down=bias_down, cotangent=cotangent)


NORM_EPS = 1e-05
GELU_COEF = math.sqrt(2.0 / math.pi)

def layer_norm_forward(residual_state, norm_gain, norm_shift):
    center = residual_state - lax.optimization_barrier(jnp.mean(residual_state, axis=-1, keepdims=True))
    inv_std = lax.rsqrt(lax.optimization_barrier(jnp.mean(center * center, axis=-1, keepdims=True)) + NORM_EPS)
    normed = center * inv_std
    return (normed * norm_gain.astype(jnp.float32) + norm_shift.astype(jnp.float32), normed, inv_std)

def layer_norm_backward(grad_norm, normed, inv_std, norm_gain):
    scaled = grad_norm * norm_gain.astype(jnp.float32)
    return inv_std * (scaled - lax.optimization_barrier(jnp.mean(scaled, axis=-1, keepdims=True)) - normed * lax.optimization_barrier(jnp.mean(scaled * normed, axis=-1, keepdims=True)))

def gelu_parts(pre_act):
    inner_arg = GELU_COEF * (pre_act + 0.044715 * pre_act * pre_act * pre_act)
    tangent = jnp.tanh(inner_arg)
    gelu_value = 0.5 * pre_act * (1.0 + tangent)
    gelu_slope = 0.5 * (1.0 + tangent) + 0.5 * pre_act * (1.0 - tangent * tangent) * GELU_COEF * (1.0 + 3.0 * 0.044715 * pre_act * pre_act)
    return (gelu_value, gelu_slope)

def split_heads(matrix):
    return matrix.reshape(matrix.shape[0], HEADS, HEAD_DIM).astype(jnp.float32)

def masked_scores(queries, keys_all):
    raw_scores = jnp.einsum('qhd,khd->hqk', split_heads(queries), split_heads(keys_all)) * HEAD_DIM ** (-0.5)
    query_pos = jnp.arange(queries.shape[0], dtype=jnp.int32)
    key_pos = jnp.arange(keys_all.shape[0], dtype=jnp.int32)
    allowed = key_pos[None, :] <= query_pos[:, None]
    return jnp.where(allowed[None], raw_scores, jnp.float32(-1e+30))

def one_sequence(params, residual_state, output_gradient):
    first_norm_gain, first_norm_bias, w_qkv, bias_q, bias_v, w_out, bias_out, second_norm_gain, second_norm_bias, w_up, bias_up, w_down, bias_down = params
    width = residual_state.shape[1]
    rows = residual_state.shape[0]
    first_normalized, first_standardized, first_inverse_deviation = layer_norm_forward(residual_state, first_norm_gain, first_norm_bias)
    act_one = first_normalized.astype(jnp.bfloat16)
    projected = jnp.dot(act_one, w_qkv, preferred_element_type=jnp.float32)
    queries = (projected[:, :width] + bias_q.astype(jnp.float32)).astype(jnp.bfloat16)
    keys_all = projected[:, width:2 * width].astype(jnp.bfloat16)
    values_all = (projected[:, 2 * width:] + bias_v.astype(jnp.float32)).astype(jnp.bfloat16)
    scores = masked_scores(queries, keys_all)
    row_max = lax.optimization_barrier(jnp.max(scores, axis=-1, keepdims=True))
    log_total = row_max + jnp.log(lax.optimization_barrier(jnp.sum(jnp.exp(scores - row_max), axis=-1, keepdims=True)))
    prob_b = jnp.exp(scores - log_total).astype(jnp.bfloat16)
    context = jnp.einsum('hqk,khd->qhd', prob_b.astype(jnp.float32), split_heads(values_all)).reshape(rows, width).astype(jnp.bfloat16)
    midpoint_state = residual_state + jnp.dot(context, w_out, preferred_element_type=jnp.float32) + bias_out.astype(jnp.float32)
    second_normalized, second_standardized, second_inverse_deviation = layer_norm_forward(midpoint_state, second_norm_gain, second_norm_bias)
    act_two = second_normalized.astype(jnp.bfloat16)
    pre_act = jnp.dot(act_two, w_up, preferred_element_type=jnp.float32) + bias_up.astype(jnp.float32)
    gelu_value, gelu_slope = gelu_parts(pre_act)
    hidden = gelu_value.astype(jnp.bfloat16)
    result = midpoint_state + jnp.dot(hidden, w_down, preferred_element_type=jnp.float32) + bias_down.astype(jnp.float32)
    cot_b = output_gradient.astype(jnp.bfloat16)
    d_w_down = jnp.dot(hidden.T, cot_b, preferred_element_type=jnp.float32)
    d_bias_down = lax.optimization_barrier(jnp.sum(output_gradient, axis=0))
    grad_pre = jnp.dot(cot_b, w_down.T, preferred_element_type=jnp.float32) * gelu_slope
    grad_pre_b = grad_pre.astype(jnp.bfloat16)
    d_w_up = jnp.dot(act_two.T, grad_pre_b, preferred_element_type=jnp.float32)
    d_bias_up = lax.optimization_barrier(jnp.sum(grad_pre, axis=0))
    second_activation_gradient = jnp.dot(grad_pre_b, w_up.T, preferred_element_type=jnp.float32)
    second_norm_gain_gradient = lax.optimization_barrier(jnp.sum(second_activation_gradient * second_standardized, axis=0))
    d_ln2_bias = lax.optimization_barrier(jnp.sum(second_activation_gradient, axis=0))
    midpoint_gradient = output_gradient + layer_norm_backward(second_activation_gradient, second_standardized, second_inverse_deviation, second_norm_gain)
    grad_mid_b = midpoint_gradient.astype(jnp.bfloat16)
    d_w_out = jnp.dot(context.T, grad_mid_b, preferred_element_type=jnp.float32)
    d_bias_out = lax.optimization_barrier(jnp.sum(midpoint_gradient, axis=0))
    grad_context = jnp.dot(grad_mid_b, w_out.T, preferred_element_type=jnp.float32).astype(jnp.bfloat16)
    attn_prob = jnp.exp(scores - log_total)
    grad_prob = jnp.einsum('qhd,khd->hqk', split_heads(grad_context), split_heads(values_all))
    grad_score = (attn_prob * (grad_prob - lax.optimization_barrier(jnp.sum(attn_prob * grad_prob, axis=-1, keepdims=True))) * HEAD_DIM ** (-0.5)).astype(jnp.bfloat16)
    grad_queries = jnp.einsum('hqk,khd->qhd', grad_score.astype(jnp.float32), split_heads(keys_all)).reshape(rows, width)
    grad_keys = jnp.einsum('hqk,qhd->khd', grad_score.astype(jnp.float32), split_heads(queries)).reshape(rows, width)
    grad_values = jnp.einsum('hqk,qhd->khd', prob_b.astype(jnp.float32), split_heads(grad_context)).reshape(rows, width)
    d_bias_q = lax.optimization_barrier(jnp.sum(grad_queries, axis=0))
    d_bias_v = lax.optimization_barrier(jnp.sum(grad_values, axis=0))
    grad_proj = jnp.concatenate([grad_queries, grad_keys, grad_values], axis=1).astype(jnp.bfloat16)
    d_w_qkv = jnp.dot(act_one.T, grad_proj, preferred_element_type=jnp.float32)
    first_activation_gradient = jnp.dot(grad_proj, w_qkv.T, preferred_element_type=jnp.float32)
    first_norm_gain_gradient = lax.optimization_barrier(jnp.sum(first_activation_gradient * first_standardized, axis=0))
    d_ln1_bias = lax.optimization_barrier(jnp.sum(first_activation_gradient, axis=0))
    input_gradient = midpoint_gradient + layer_norm_backward(first_activation_gradient, first_standardized, first_inverse_deviation, first_norm_gain)
    grads = (first_norm_gain_gradient, d_ln1_bias, d_w_qkv, d_bias_q, d_bias_v, d_w_out, d_bias_out, second_norm_gain_gradient, d_ln2_bias, d_w_up, d_bias_up, d_w_down, d_bias_down)
    return (result, input_gradient, grads)

def reference(stream_in, first_norm_gain, first_norm_bias, w_qkv, bias_q, bias_v, w_out, bias_out, second_norm_gain, second_norm_bias, w_up, bias_up, w_down, bias_down, cotangent):
    params = (first_norm_gain, first_norm_bias, w_qkv, bias_q, bias_v, w_out, bias_out, second_norm_gain, second_norm_bias, w_up, bias_up, w_down, bias_down)
    zero_grads = tuple((jnp.zeros(param_one.shape, jnp.float32) for param_one in params))

    def seq_step(carry, item):
        residual_state, output_gradient = item
        result, input_gradient, grads = one_sequence(params, residual_state, output_gradient)
        return (tuple((total + grad_one for total, grad_one in zip(carry, grads))), (result, input_gradient))
    totals, outputs = lax.scan(seq_step, zero_grads, (stream_in, cotangent))
    return (outputs[0], outputs[1], totals[0], totals[1], totals[2], totals[3], totals[4], totals[5], totals[6], totals[7], totals[8], totals[9], totals[10], totals[11], totals[12])
```

```python
import functools
import math

import jax
import jax.numpy as jnp
from jax import lax
from jax.experimental import pallas as pl
from jax.experimental.pallas import tpu as pltpu
from jax.sharding import PartitionSpec as P

HEADS = 16
HEAD_DIM = 64
BF = jnp.bfloat16
F32 = jnp.float32

NORM_EPS = 1e-05
GELU_COEF = math.sqrt(2.0 / math.pi)


def layer_norm_forward(residual_state, norm_gain, norm_shift):
    center = residual_state - jnp.mean(residual_state, axis=-1, keepdims=True)
    inv_std = lax.rsqrt(jnp.mean(center * center, axis=-1, keepdims=True) + NORM_EPS)
    normed = center * inv_std
    return (
        normed * norm_gain.astype(jnp.float32) + norm_shift.astype(jnp.float32),
        normed,
        inv_std,
    )


def layer_norm_backward(grad_norm, normed, inv_std, norm_gain):
    scaled = grad_norm * norm_gain.astype(jnp.float32)
    return inv_std * (
        scaled
        - jnp.mean(scaled, axis=-1, keepdims=True)
        - normed * jnp.mean(scaled * normed, axis=-1, keepdims=True)
    )


def gelu_parts(pre_act):
    inner_arg = GELU_COEF * (pre_act + 0.044715 * pre_act * pre_act * pre_act)
    tangent = jnp.tanh(inner_arg)
    gelu_value = 0.5 * pre_act * (1.0 + tangent)
    gelu_slope = 0.5 * (1.0 + tangent) + 0.5 * pre_act * (1.0 - tangent * tangent) * GELU_COEF * (
        1.0 + 3.0 * 0.044715 * pre_act * pre_act
    )
    return (gelu_value, gelu_slope)


def contract(x, y, dx, dy):
    return lax.dot_general(x, y, (((dx,), (dy,)), ((), ())), preferred_element_type=F32)


def probabilities(q, k, row_pos, col_pos):
    scores = contract(q, k, 1, 1) * HEAD_DIM ** (-0.5)
    scores = jnp.where(col_pos <= row_pos, scores, F32(-1e30))
    row_max = jnp.max(scores, axis=-1, keepdims=True)
    total = jnp.sum(jnp.exp(scores - row_max), axis=-1, keepdims=True)
    return jnp.exp(scores - (row_max + jnp.log(total)))


def forward_kernel(row_ref, col_ref, q_ref, k_ref, v_ref, ctx_ref):
    row_pos, col_pos = row_ref[...], col_ref[...]
    outs = []
    for lo in range(0, q_ref.shape[1], HEAD_DIM):
        head = slice(lo, lo + HEAD_DIM)
        prob = probabilities(q_ref[:, head], k_ref[:, head], row_pos, col_pos)
        outs.append(contract(prob.astype(BF), v_ref[:, head], 1, 0))
    ctx_ref[...] = jnp.concatenate(outs, axis=1).astype(BF)


def backward_kernel(
    row_ref, col_ref, q_ref, k_ref, v_ref, g_ref, dq_ref, dk_ref, dv_ref, bq_ref, bv_ref
):
    row_pos, col_pos = row_ref[...], col_ref[...]
    dq, dk, dv = [], [], []
    for lo in range(0, q_ref.shape[1], HEAD_DIM):
        head = slice(lo, lo + HEAD_DIM)
        q, k, v, g = q_ref[:, head], k_ref[:, head], v_ref[:, head], g_ref[:, head]
        prob = probabilities(q, k, row_pos, col_pos)
        grad_prob = contract(g, v, 1, 1)
        mean = jnp.sum(prob * grad_prob, axis=-1, keepdims=True)
        grad_score = (prob * (grad_prob - mean) * HEAD_DIM ** (-0.5)).astype(BF)
        dq.append(contract(grad_score, k, 1, 0))
        dk.append(contract(grad_score, q, 0, 0))
        dv.append(contract(prob.astype(BF), g, 0, 0))
    dq, dk, dv = (jnp.concatenate(part, axis=1) for part in (dq, dk, dv))
    dq_ref[...] = dq.astype(BF)
    dk_ref[...] = dk.astype(BF)
    dv_ref[...] = dv.astype(BF)
    bq_ref[...] = jnp.sum(dq, axis=0, keepdims=True)
    bv_ref[...] = jnp.sum(dv, axis=0, keepdims=True)


def attention_call(kernel, row_pos, col_pos, arrays, outs):
    tokens, width = arrays[0].shape
    block = 2 * HEAD_DIM if width % (2 * HEAD_DIM) == 0 else width

    def spec(rows):
        return pl.BlockSpec((rows, block), lambda i: (0, i))

    return pl.pallas_call(
        kernel,
        grid=(width // block,),
        in_specs=[
            pl.BlockSpec((tokens, 1), lambda i: (0, 0)),
            pl.BlockSpec((1, tokens), lambda i: (0, 0)),
        ]
        + [spec(tokens)] * len(arrays),
        out_specs=[spec(o[0]) for o in outs],
        out_shape=[jax.ShapeDtypeStruct((o[0], width), o[1]) for o in outs],
        compiler_params=pltpu.CompilerParams(vmem_limit_bytes=60 * 1024 * 1024),
        cost_estimate=pl.CostEstimate(
            flops=4 * len(arrays) * tokens * tokens * width,
            bytes_accessed=4 * len(arrays) * tokens * width,
            transcendentals=2 * tokens * tokens * width // HEAD_DIM,
        ),
    )(row_pos, col_pos, *arrays)


def per_device(
    stream_in,
    first_norm_gain,
    first_norm_bias,
    w_qkv,
    bias_q,
    bias_v,
    w_out,
    bias_out,
    second_norm_gain,
    second_norm_bias,
    w_up,
    bias_up,
    w_down,
    bias_down,
    cotangent,
):
    group = lax.axis_size("grp")
    me = lax.axis_index("grp")
    residual = stream_in[0]
    cot = cotangent[0]
    rows, width = residual.shape
    cols = width // group
    tokens = rows * group
    hid = w_up.shape[1] // group

    def other(r):
        return lax.rem(me + (r % group), group)

    def send(x, shift):
        return lax.ppermute(x, "grp", [(i, (i + shift) % group) for i in range(group)])

    def roll(x, r):
        r = (r % group) * rows
        return x if r == 0 else jnp.concatenate([x[r:], x[:r]], axis=0)

    def block(x, r):
        return x[r * rows : (r + 1) * rows]

    def column_block(x, index, size):
        return lax.dynamic_slice_in_dim(x, index * size, size, axis=1)

    def gather_rows(x):
        return jnp.concatenate([x] + [send(x, -r) for r in range(1, group)], axis=0)

    def rows_to_columns(x):
        parts = [column_block(x, me, cols)]
        parts += [send(column_block(x, other(-r), cols), -r) for r in range(1, group)]
        return jnp.concatenate(parts, axis=0)

    def sum_columns(x, weight_of):
        received = [
            send(contract(roll(x, r), weight_of(other(r)), 1, 0).astype(BF), r)
            for r in range(1, group)
        ]
        total = contract(x, weight_of(me), 1, 0)
        for part in received:
            total = total + part.astype(F32)
        return total

    def sum_rows(x, weight):
        received = [
            send(contract(block(x, r), weight, 1, 0).astype(BF), r) for r in range(1, group)
        ]
        total = contract(block(x, 0), weight, 1, 0)
        for part in received:
            total = total + part.astype(F32)
        return total

    def columns_to_rows(x):
        whole = jnp.zeros((rows, width), F32)
        whole = lax.dynamic_update_slice_in_dim(whole, block(x, 0), me * cols, axis=1)
        for r in range(1, group):
            part = send(block(x, r).astype(BF), r).astype(F32)
            whole = lax.dynamic_update_slice_in_dim(whole, part, other(-r) * cols, axis=1)
        return whole

    def gather_columns(x):
        parts = [x] + [send(roll(x, -r), -r) for r in range(1, group)]
        if group == 2:
            low = jnp.where(me == 0, parts[0], parts[1])
            high = jnp.where(me == 0, parts[1], parts[0])
            return jnp.stack([low, high], axis=-2)
        whole = jnp.zeros(x.shape[:-1] + (group, x.shape[-1]), x.dtype)
        for r, part in enumerate(parts):
            whole = lax.dynamic_update_slice_in_dim(
                whole, jnp.expand_dims(part, -2), other(r), axis=x.ndim - 1
            )
        return whole

    cot_b = cot.astype(BF)
    cot_full = gather_rows(cot_b)
    vectors = jnp.stack(
        [first_norm_gain, first_norm_bias, second_norm_gain, second_norm_bias, bias_out, bias_down]
    )
    vectors = lax.all_gather(vectors, "grp", axis=1, tiled=True)
    gain_one, shift_one, gain_two, shift_two, full_bo, full_bd = (vectors[i] for i in range(6))

    normalized, standard_one, inverse_one = layer_norm_forward(residual, gain_one, shift_one)
    act_one_cols = rows_to_columns(normalized.astype(BF))
    w3 = w_qkv.reshape(cols, 3, group, cols)
    qkv = sum_columns(
        act_one_cols,
        lambda d: lax.dynamic_index_in_dim(w3, d, axis=2, keepdims=False).reshape(cols, 3 * cols),
    )
    queries = (qkv[:, :cols] + bias_q.astype(F32)).astype(BF)
    keys = qkv[:, cols : 2 * cols].astype(BF)
    values = (qkv[:, 2 * cols :] + bias_v.astype(F32)).astype(BF)

    index = jnp.arange(tokens, dtype=jnp.int32)
    position = lax.rem(index + me * rows, tokens)
    row_pos, col_pos = position[:, None], position[None, :]
    (context,) = attention_call(
        forward_kernel, row_pos, col_pos, (queries, keys, values), [(tokens, BF)]
    )
    middle = residual + sum_rows(context, w_out) + full_bo.astype(F32)

    normalized, standard_two, inverse_two = layer_norm_forward(middle, gain_two, shift_two)
    act_two_cols = rows_to_columns(normalized.astype(BF))
    pre_act = sum_columns(act_two_cols, lambda d: column_block(w_up, d, hid)) + bias_up.astype(F32)
    gelu_value, gelu_slope = gelu_parts(pre_act)
    hidden = gelu_value.astype(BF)

    grad_pre = contract(cot_full, w_down, 1, 1) * gelu_slope
    grad_pre_b = grad_pre.astype(BF)
    d_bias_up = jnp.sum(grad_pre, axis=0)
    grad_pre_full = gather_columns(grad_pre_b).reshape(tokens, group * hid)
    d_w_down = contract(hidden, cot_full, 0, 0)
    total_w_down = lax.psum(d_w_down.astype(BF), "rep")
    result = middle + sum_rows(hidden, w_down) + full_bd.astype(F32)

    grad_act_cols = contract(grad_pre_full, w_up, 1, 1)
    d_shift_two = jnp.sum(grad_act_cols, axis=0)
    grad_act = columns_to_rows(grad_act_cols)
    d_w_up = contract(act_two_cols, grad_pre_full, 0, 0)
    total_w_up = lax.psum(d_w_up.astype(BF), "rep")
    d_gain_two = jnp.sum(grad_act * standard_two, axis=0)
    grad_middle = cot + layer_norm_backward(grad_act, standard_two, inverse_two, gain_two)

    grad_mid_full = gather_rows(grad_middle.astype(BF))
    grad_context = contract(grad_mid_full, w_out, 1, 1).astype(BF)
    d_w_out = contract(context, grad_mid_full, 0, 0)
    d_q, d_k, d_v, d_bias_q, d_bias_v = attention_call(
        backward_kernel,
        row_pos,
        col_pos,
        (queries, keys, values, grad_context),
        [(tokens, BF)] * 3 + [(1, F32)] * 2,
    )
    grad_proj = jnp.stack([d_q, d_k, d_v], axis=1)
    grad_proj_full = gather_columns(grad_proj).reshape(tokens, 3 * group * cols)
    grad_act_cols = contract(grad_proj_full, w_qkv, 1, 1)
    d_shift_one = jnp.sum(grad_act_cols, axis=0)
    grad_act = columns_to_rows(grad_act_cols)
    d_w_qkv = contract(act_one_cols, grad_proj_full, 0, 0)
    d_gain_one = jnp.sum(grad_act * standard_one, axis=0)
    input_gradient = grad_middle + layer_norm_backward(
        grad_act, standard_one, inverse_one, gain_one
    )
    total_w_out = lax.psum(d_w_out.astype(BF), "rep")
    total_w_qkv = lax.psum(d_w_qkv.astype(BF), "rep")

    sums = jnp.stack(
        [d_gain_one, d_gain_two, jnp.sum(grad_middle, axis=0), jnp.sum(cot, axis=0)]
    )
    mine = column_block(sums, me, cols)
    for r in range(1, group):
        mine = mine + send(column_block(sums, other(r), cols), r)
    owned = jnp.stack([d_shift_one, d_shift_two, d_bias_q[0], d_bias_v[0]])
    small = jnp.concatenate([mine.reshape(-1), owned.reshape(-1), d_bias_up])
    small = lax.psum(small, "rep")
    part = [small[i * cols : (i + 1) * cols] for i in range(8)]
    return (
        result[None],
        input_gradient[None],
        part[0],
        part[4],
        total_w_qkv.astype(F32),
        part[6],
        part[7],
        total_w_out.astype(F32),
        part[2],
        part[1],
        part[5],
        total_w_up.astype(F32),
        small[8 * cols :],
        total_w_down.astype(F32),
        part[3],
    )


def solution(mesh):
    return jax.shard_map(
        per_device,
        mesh=mesh,
        in_specs=(
            P("rep", "grp", None),
            P("grp"),
            P("grp"),
            P("grp", None),
            P("grp"),
            P("grp"),
            P("grp", None),
            P("grp"),
            P("grp"),
            P("grp"),
            P("grp", None),
            P("grp"),
            P("grp", None),
            P("grp"),
            P("rep", "grp", None),
        ),
        out_specs=(
            P("rep", "grp", None),
            P("rep", "grp", None),
            P("grp"),
            P("grp"),
            P("grp", None),
            P("grp"),
            P("grp"),
            P("grp", None),
            P("grp"),
            P("grp"),
            P("grp"),
            P("grp", None),
            P("grp"),
            P("grp", None),
            P("grp"),
        ),
        check_vma=False,
    )
```

```python
import math

import jax
import jax.numpy as jnp
from jax import lax
from jax.experimental import pallas as pl
from jax.experimental.pallas import tpu as pltpu
from jax.sharding import PartitionSpec as P


HEADS = 16
HEAD_DIM = 64
BF = jnp.bfloat16
F32 = jnp.float32

NORM_EPS = 1e-05
GELU_COEF = math.sqrt(2.0 / math.pi)


def layer_norm_forward(residual_state, norm_gain, norm_shift):
    center = residual_state - jnp.mean(residual_state, axis=-1, keepdims=True)
    inv_std = lax.rsqrt(jnp.mean(center * center, axis=-1, keepdims=True) + NORM_EPS)
    normed = center * inv_std
    return (
        normed * norm_gain.astype(jnp.float32) + norm_shift.astype(jnp.float32),
        normed,
        inv_std,
    )


def layer_norm_backward(grad_norm, normed, inv_std, norm_gain):
    scaled = grad_norm * norm_gain.astype(jnp.float32)
    return inv_std * (
        scaled
        - jnp.mean(scaled, axis=-1, keepdims=True)
        - normed * jnp.mean(scaled * normed, axis=-1, keepdims=True)
    )


def gelu_parts(pre_act):
    inner_arg = GELU_COEF * (pre_act + 0.044715 * pre_act * pre_act * pre_act)
    tangent = jnp.tanh(inner_arg)
    gelu_value = 0.5 * pre_act * (1.0 + tangent)
    gelu_slope = 0.5 * (1.0 + tangent) + 0.5 * pre_act * (1.0 - tangent * tangent) * GELU_COEF * (
        1.0 + 3.0 * 0.044715 * pre_act * pre_act
    )
    return (gelu_value, gelu_slope)


def contract(x, y, dx, dy):
    return lax.dot_general(x, y, (((dx,), (dy,)), ((), ())), preferred_element_type=F32)


def probabilities(q, k, row_pos, col_pos):
    scores = contract(q, k, 1, 1) * HEAD_DIM ** (-0.5)
    scores = jnp.where(col_pos <= row_pos, scores, F32(-1e30))
    row_max = jnp.max(scores, axis=-1, keepdims=True)
    total = jnp.sum(jnp.exp(scores - row_max), axis=-1, keepdims=True)
    return jnp.exp(scores - (row_max + jnp.log(total)))


def forward_kernel(row_ref, col_ref, q_ref, k_ref, v_ref, ctx_ref):
    row_pos, col_pos = row_ref[...], col_ref[...]
    outs = []
    for lo in range(0, q_ref.shape[1], HEAD_DIM):
        head = slice(lo, lo + HEAD_DIM)
        prob = probabilities(q_ref[:, head], k_ref[:, head], row_pos, col_pos)
        outs.append(contract(prob.astype(BF), v_ref[:, head], 1, 0))
    ctx_ref[...] = jnp.concatenate(outs, axis=1).astype(BF)


def backward_kernel(
    row_ref, col_ref, q_ref, k_ref, v_ref, g_ref, dq_ref, dk_ref, dv_ref, bq_ref, bv_ref
):
    row_pos, col_pos = row_ref[...], col_ref[...]
    dq, dk, dv = [], [], []
    for lo in range(0, q_ref.shape[1], HEAD_DIM):
        head = slice(lo, lo + HEAD_DIM)
        q, k, v, g = q_ref[:, head], k_ref[:, head], v_ref[:, head], g_ref[:, head]
        prob = probabilities(q, k, row_pos, col_pos)
        grad_prob = contract(g, v, 1, 1)
        mean = jnp.sum(prob * grad_prob, axis=-1, keepdims=True)
        grad_score = (prob * (grad_prob - mean) * HEAD_DIM ** (-0.5)).astype(BF)
        dq.append(contract(grad_score, k, 1, 0))
        dk.append(contract(grad_score, q, 0, 0))
        dv.append(contract(prob.astype(BF), g, 0, 0))
    dq, dk, dv = (jnp.concatenate(part, axis=1) for part in (dq, dk, dv))
    dq_ref[...] = dq.astype(BF)
    dk_ref[...] = dk.astype(BF)
    dv_ref[...] = dv.astype(BF)
    bq_ref[...] = jnp.sum(dq, axis=0, keepdims=True)
    bv_ref[...] = jnp.sum(dv, axis=0, keepdims=True)


def attention_call(kernel, row_pos, col_pos, arrays, outs):
    tokens, width = arrays[0].shape
    block = 2 * HEAD_DIM if width % (2 * HEAD_DIM) == 0 else width

    def spec(rows):
        return pl.BlockSpec((rows, block), lambda i: (0, i))

    return pl.pallas_call(
        kernel,
        grid=(width // block,),
        in_specs=[
            pl.BlockSpec((tokens, 1), lambda i: (0, 0)),
            pl.BlockSpec((1, tokens), lambda i: (0, 0)),
        ]
        + [spec(tokens)] * len(arrays),
        out_specs=[spec(o[0]) for o in outs],
        out_shape=[jax.ShapeDtypeStruct((o[0], width), o[1]) for o in outs],
        compiler_params=pltpu.CompilerParams(vmem_limit_bytes=60 * 1024 * 1024),
        cost_estimate=pl.CostEstimate(
            flops=4 * len(arrays) * tokens * tokens * width,
            bytes_accessed=4 * len(arrays) * tokens * width,
            transcendentals=2 * tokens * tokens * width // HEAD_DIM,
        ),
    )(row_pos, col_pos, *arrays)


def paired_sum(small):
    size = lax.axis_size("rep")
    if size & (size - 1):
        return lax.psum(small, "rep")
    step = 1
    while step < size:
        small = small + lax.ppermute(small, "rep", [(i, i ^ step) for i in range(size)])
        step *= 2
    return small


def ring_sum(arrays):
    size = lax.axis_size("rep")
    chips = size // 2
    rows = arrays[0].shape[0]
    piece = rows // (4 * chips)
    if size % 2 or rows != 4 * chips * piece:
        return [lax.psum(a.astype(BF), "rep").astype(F32) for a in arrays]
    order = [c for c in range(0, chips, 2)] + [c for c in range(chips - 1, -1, -1) if c % 2]
    me = lax.axis_index("rep")
    core = lax.rem(me, 2)
    chip = me // 2
    place = jnp.where(lax.rem(chip, 2) == 0, chip // 2, chips - 1 - chip // 2)
    half = rows // 2

    swap = [(i, i ^ 1) for i in range(size)]
    ahead = [
        (order[i] * 2 + c, order[(i + 1) % chips] * 2 + c) for i in range(chips) for c in range(2)
    ]
    back = [(b, a) for a, b in ahead]

    def rows_of(a, start, count):
        return lax.dynamic_slice_in_dim(a, start, count, axis=0)

    theirs = [rows_of(a, (1 - core) * half, half).astype(BF) for a in arrays]
    mine = [
        rows_of(a, core * half, half).astype(F32) + lax.ppermute(t, "rep", swap).astype(F32)
        for a, t in zip(arrays, theirs)
    ]
    mine = [m.astype(BF) for m in mine]
    share = jnp.concatenate(mine, axis=1) if len(mine) > 1 else mine[0]

    def index(side, k):
        return (side * chips + lax.rem(place + (k % chips), chips)) * piece

    held = [rows_of(share, index(0, -1), piece), rows_of(share, index(1, 1), piece)]
    for t in range(chips - 1):
        held = [lax.ppermute(held[0], "rep", ahead), lax.ppermute(held[1], "rep", back)]
        local = [
            rows_of(share, index(0, -2 - t), piece),
            rows_of(share, index(1, 2 + t), piece),
        ]
        held = [(h.astype(F32) + x.astype(F32)).astype(BF) for h, x in zip(held, local)]
    whole = jnp.zeros(share.shape, BF)
    for t in range(chips):
        if t:
            held = [lax.ppermute(held[0], "rep", ahead), lax.ppermute(held[1], "rep", back)]
        whole = lax.dynamic_update_slice_in_dim(whole, held[0], index(0, -t), axis=0)
        whole = lax.dynamic_update_slice_in_dim(whole, held[1], index(1, t), axis=0)
    partner = lax.ppermute(whole, "rep", swap)
    low = jnp.where(core == 0, whole, partner)
    high = jnp.where(core == 0, partner, whole)
    total = jnp.concatenate([low, high], axis=0).astype(F32)
    outs, at = [], 0
    for a in arrays:
        outs.append(total[:, at : at + a.shape[1]])
        at += a.shape[1]
    return outs


def per_device(
    stream_in,
    first_norm_gain,
    first_norm_bias,
    w_qkv,
    bias_q,
    bias_v,
    w_out,
    bias_out,
    second_norm_gain,
    second_norm_bias,
    w_up,
    bias_up,
    w_down,
    bias_down,
    cotangent,
):
    group = lax.axis_size("grp")
    me = lax.axis_index("grp")
    residual = stream_in[0]
    cot = cotangent[0]
    rows, width = residual.shape
    cols = width // group
    tokens = rows * group
    hid = w_up.shape[1] // group

    def other(r):
        return lax.rem(me + (r % group), group)

    def send(x, shift):
        return lax.ppermute(x, "grp", [(i, (i + shift) % group) for i in range(group)])

    def roll(x, r):
        r = (r % group) * rows
        return x if r == 0 else jnp.concatenate([x[r:], x[:r]], axis=0)

    def block(x, r):
        return x[r * rows : (r + 1) * rows]

    def column_block(x, index, size):
        return lax.dynamic_slice_in_dim(x, index * size, size, axis=1)

    def gather_rows(x):
        return jnp.concatenate([x] + [send(x, -r) for r in range(1, group)], axis=0)

    def rows_to_columns(x):
        parts = [column_block(x, me, cols)]
        parts += [send(column_block(x, other(-r), cols), -r) for r in range(1, group)]
        return jnp.concatenate(parts, axis=0)

    def sum_columns(x, weight_of):
        received = [
            send(contract(roll(x, r), weight_of(other(r)), 1, 0).astype(BF), r)
            for r in range(1, group)
        ]
        total = contract(x, weight_of(me), 1, 0)
        for part in received:
            total = total + part.astype(F32)
        return total

    def sum_rows(x, weight):
        received = [
            send(contract(block(x, r), weight, 1, 0).astype(BF), r) for r in range(1, group)
        ]
        total = contract(block(x, 0), weight, 1, 0)
        for part in received:
            total = total + part.astype(F32)
        return total

    def columns_to_rows(x):
        whole = jnp.zeros((rows, width), F32)
        whole = lax.dynamic_update_slice_in_dim(whole, block(x, 0), me * cols, axis=1)
        for r in range(1, group):
            part = send(block(x, r).astype(BF), r).astype(F32)
            whole = lax.dynamic_update_slice_in_dim(whole, part, other(-r) * cols, axis=1)
        return whole

    def gather_columns(x):
        parts = [x] + [send(roll(x, -r), -r) for r in range(1, group)]
        if group == 2:
            low = jnp.where(me == 0, parts[0], parts[1])
            high = jnp.where(me == 0, parts[1], parts[0])
            return jnp.stack([low, high], axis=-2)
        whole = jnp.zeros(x.shape[:-1] + (group, x.shape[-1]), x.dtype)
        for r, part in enumerate(parts):
            whole = lax.dynamic_update_slice_in_dim(
                whole, jnp.expand_dims(part, -2), other(r), axis=x.ndim - 1
            )
        return whole

    cot_b = cot.astype(BF)
    cot_full = gather_rows(cot_b)
    vectors = jnp.stack(
        [first_norm_gain, first_norm_bias, second_norm_gain, second_norm_bias, bias_out, bias_down]
    )
    vectors = lax.all_gather(vectors, "grp", axis=1, tiled=True)
    gain_one, shift_one, gain_two, shift_two, full_bo, full_bd = (vectors[i] for i in range(6))

    normalized, standard_one, inverse_one = layer_norm_forward(residual, gain_one, shift_one)
    act_one_cols = rows_to_columns(normalized.astype(BF))
    w3 = w_qkv.reshape(cols, 3, group, cols)
    qkv = sum_columns(
        act_one_cols,
        lambda d: lax.dynamic_index_in_dim(w3, d, axis=2, keepdims=False).reshape(cols, 3 * cols),
    )
    queries = (qkv[:, :cols] + bias_q.astype(F32)).astype(BF)
    keys = qkv[:, cols : 2 * cols].astype(BF)
    values = (qkv[:, 2 * cols :] + bias_v.astype(F32)).astype(BF)

    index = jnp.arange(tokens, dtype=jnp.int32)
    position = lax.rem(index + me * rows, tokens)
    row_pos, col_pos = position[:, None], position[None, :]
    (context,) = attention_call(
        forward_kernel, row_pos, col_pos, (queries, keys, values), [(tokens, BF)]
    )
    middle = residual + sum_rows(context, w_out) + full_bo.astype(F32)

    normalized, standard_two, inverse_two = layer_norm_forward(middle, gain_two, shift_two)
    act_two_cols = rows_to_columns(normalized.astype(BF))
    pre_act = sum_columns(act_two_cols, lambda d: column_block(w_up, d, hid)) + bias_up.astype(F32)
    gelu_value, gelu_slope = gelu_parts(pre_act)
    hidden = gelu_value.astype(BF)

    grad_pre = contract(cot_full, w_down, 1, 1) * gelu_slope
    grad_pre_b = grad_pre.astype(BF)
    d_bias_up = jnp.sum(grad_pre, axis=0)
    grad_pre_full = gather_columns(grad_pre_b).reshape(tokens, group * hid)
    d_w_down = contract(hidden, cot_full, 0, 0)
    (total_w_down,) = ring_sum([d_w_down])
    result = middle + sum_rows(hidden, w_down) + full_bd.astype(F32)

    grad_act_cols = contract(grad_pre_full, w_up, 1, 1)
    d_shift_two = jnp.sum(grad_act_cols, axis=0)
    grad_act = columns_to_rows(grad_act_cols)
    d_w_up = contract(act_two_cols, grad_pre_full, 0, 0)
    (total_w_up,) = ring_sum([d_w_up])
    d_gain_two = jnp.sum(grad_act * standard_two, axis=0)
    grad_middle = cot + layer_norm_backward(grad_act, standard_two, inverse_two, gain_two)

    grad_mid_full = gather_rows(grad_middle.astype(BF))
    grad_context = contract(grad_mid_full, w_out, 1, 1).astype(BF)
    d_w_out = contract(context, grad_mid_full, 0, 0)
    d_q, d_k, d_v, d_bias_q, d_bias_v = attention_call(
        backward_kernel,
        row_pos,
        col_pos,
        (queries, keys, values, grad_context),
        [(tokens, BF)] * 3 + [(1, F32)] * 2,
    )
    grad_proj = jnp.stack([d_q, d_k, d_v], axis=1)
    grad_proj_full = gather_columns(grad_proj).reshape(tokens, 3 * group * cols)
    grad_act_cols = contract(grad_proj_full, w_qkv, 1, 1)
    d_shift_one = jnp.sum(grad_act_cols, axis=0)
    grad_act = columns_to_rows(grad_act_cols)
    d_w_qkv = contract(act_one_cols, grad_proj_full, 0, 0)
    d_gain_one = jnp.sum(grad_act * standard_one, axis=0)
    input_gradient = grad_middle + layer_norm_backward(
        grad_act, standard_one, inverse_one, gain_one
    )
    total_w_qkv, total_w_out = ring_sum([d_w_qkv, d_w_out])

    sums = jnp.stack(
        [d_gain_one, d_gain_two, jnp.sum(grad_middle, axis=0), jnp.sum(cot, axis=0)]
    )
    mine = column_block(sums, me, cols)
    for r in range(1, group):
        mine = mine + send(column_block(sums, other(r), cols), r)
    owned = jnp.stack([d_shift_one, d_shift_two, d_bias_q[0], d_bias_v[0]])
    small = jnp.concatenate([mine.reshape(-1), owned.reshape(-1), d_bias_up])
    small = paired_sum(small)
    part = [small[i * cols : (i + 1) * cols] for i in range(8)]
    return (
        result[None],
        input_gradient[None],
        part[0],
        part[4],
        total_w_qkv,
        part[6],
        part[7],
        total_w_out,
        part[2],
        part[1],
        part[5],
        total_w_up,
        small[8 * cols :],
        total_w_down,
        part[3],
    )


def solution(mesh):
    return jax.shard_map(
        per_device,
        mesh=mesh,
        in_specs=(
            P("rep", "grp", None),
            P("grp"),
            P("grp"),
            P("grp", None),
            P("grp"),
            P("grp"),
            P("grp", None),
            P("grp"),
            P("grp"),
            P("grp"),
            P("grp", None),
            P("grp"),
            P("grp", None),
            P("grp"),
            P("rep", "grp", None),
        ),
        out_specs=(
            P("rep", "grp", None),
            P("rep", "grp", None),
            P("grp"),
            P("grp"),
            P("grp", None),
            P("grp"),
            P("grp"),
            P("grp", None),
            P("grp"),
            P("grp"),
            P("grp"),
            P("grp", None),
            P("grp"),
            P("grp", None),
            P("grp"),
        ),
        check_vma=False,
    )
```
